32 devices in a mesh: lat: 4 (over z), lev: 8 (over y, x, core).
Axes of the slice: x: 2, y: 2, z: 4, core: 2. Of those that a mesh axis runs over, the one named last changes fastest.
Arguments:
- spec_in: bfloat16 [8, 2, 8, 2560], P('lat', None, None, 'lev'), may hold values from -6 to 6
- legendre: bfloat16 [8, 2560, 2560], P('lat', 'lev'), may hold values from -0.125 to 0.125
- pattern: int32 [8, 20, 20], P('lat'), may hold values from 0 to 1, as said below
- deal_list: int32 [8], replicated, may hold values from 0 to 2559, as said below
- circle_lengths: int32 [2560], replicated, may hold values from 12 to 10256, as said below
- mixing: bfloat16 [8, 8], replicated, may hold values from -2 to 2
Outputs:
- spec_out: float32 [8, 2, 8, 2560], P('lat', None, None, 'lev')
The draws below stay inside these ranges and needn't reach their ends.
Inputs may be any that keep to these rules, and one draw needn't show every extreme that they name: `deal_list`: distinct wavenumbers; 0 and 2559 are always among them. pattern[m, a, b] is 1 exactly when b * 128 <= 2559 - deal_list[m] and a >= (deal_list[m] * 20) // 5120, else 0. `circle_lengths`: multiples of 4; row j holds a value between 20 + 4 j - 4 (j // 2 + 2) and 20 + 4 j, and the last row exactly 20 + 4 (2559).
All inputs are finite; a program needn't handle non-finite values.
Results may differ from the reference program's by a relative error of at most 0.0026.
Values may be sent and summed in bfloat16 or wider, within the bound.
A program may use at most 64 MiB of HBM per device.

```python
import math
import jax
import jax.numpy as jnp
from jax import lax

NLAT = 5120
NK = 2560
BLK = 128
HLAT = 2560
MW = 8
FIELDS = 8


def common_waves(key):
    first_key = jax.random.fold_in(key, 11)
    second_key = jax.random.fold_in(key, 12)
    middle = 1 + jax.random.permutation(first_key, NK - 2)[:MW - 2]
    chosen = jnp.concatenate([jnp.array([0, NK - 1], dtype=jnp.int32), middle.astype(jnp.int32)])
    return jax.random.permutation(second_key, chosen)


def draw_deal_list(key, part):
    return common_waves(key)


def draw_pattern(key, part):
    wavenums = common_waves(key)
    row_blocks = jnp.arange(HLAT // BLK, dtype=jnp.int32)
    col_blocks = jnp.arange(NK // BLK, dtype=jnp.int32)
    polar_cut = wavenums * (HLAT // BLK) // (2 * NK)
    rows_live = row_blocks[None, :] >= polar_cut[:, None]
    cols_live = col_blocks[None, :] * BLK <= (NK - 1 - wavenums)[:, None]
    return (rows_live[:, :, None] & cols_live[:, None, :]).astype(jnp.int32)


def draw_circle_lengths(key, part):
    row_ids = jnp.arange(HLAT, dtype=jnp.int32)
    upper = (row_ids // 2 + 3).astype(jnp.int32)
    dropped = jax.random.randint(jax.random.fold_in(key, 21), (HLAT,), 0, upper).astype(jnp.int32)
    dropped = jnp.where(row_ids == HLAT - 1, 0, dropped)
    return (20 + 4 * row_ids - 4 * dropped).astype(jnp.int32)


def steps_of(stream_key, shape, split, smallest, largest):
    loudness, own = 1.0, jax.random.fold_in(stream_key, 6)
    for dim, shards_of in split:
        heights = jnp.exp(jax.random.uniform(jax.random.fold_in(own, dim), (shards_of,), jnp.float32, smallest / len(split), largest / len(split)))
        loudness = loudness * jnp.repeat(heights, shape[dim] // shards_of).reshape([-1 if axis == dim else 1 for axis in range(len(shape))])
    return loudness


def normal_values(own_key, dims, spread, most, shards=(), kind=jnp.bfloat16):
    values = jax.random.normal(own_key, dims, jnp.float32) * spread
    if len(shards) > 0:
        values = steps_of(own_key, dims, shards, -0.22, 0.18) * values
    return jnp.clip(values, min=-most, max=most).astype(kind)


def setup_inputs(seed: int = 0) -> dict:
    seeds = jax.random.split(jax.random.key(seed), 7)
    spec_in = normal_values(seeds[0], (MW, 2, FIELDS, NK), 1.0, 6.0, ((0, 4), (3, 8)))
    legendre = normal_values(seeds[1], (MW, NK, HLAT), NK ** -0.5, 0.125, ((0, 4), (1, 8)))
    pattern = draw_pattern(jax.random.fold_in(seeds[6], 71), 0)
    deal_list = draw_deal_list(jax.random.fold_in(seeds[6], 71), 0)
    circle_lengths = draw_circle_lengths(jax.random.fold_in(seeds[6], 71), 0)
    mixing = normal_values(seeds[5], (FIELDS, FIELDS), FIELDS ** -0.5, 2.0)
    return {"spec_in": spec_in, "legendre": legendre, "pattern": pattern, "deal_list": deal_list, "circle_lengths": circle_lengths, "mixing": mixing}


def live_table(block_mask, dense_rows):
    expanded = jnp.repeat(jnp.repeat(block_mask, BLK, axis=0), BLK, axis=1)
    return dense_rows.astype(jnp.float32) * jnp.transpose(expanded).astype(jnp.float32)

def circle_tables(wavenums, length):
    lon_count = 20 + 4 * (HLAT - 1)
    positions = jnp.arange(lon_count, dtype=jnp.int32)
    phases = wavenums.astype(jnp.int32)[:, None] * positions[None, :] % length
    angles = phases.astype(jnp.float32) * (2.0 * math.pi) / length.astype(jnp.float32)
    inside = positions[None, :] < length
    cosine_table = jnp.where(inside, jnp.cos(angles), 0.0).astype(jnp.bfloat16)
    sine_table = jnp.where(inside, jnp.sin(angles), 0.0).astype(jnp.bfloat16)
    return (cosine_table, sine_table)

def reference(spec_in, legendre, pattern, deal_list, circle_lengths, mixing):
    parity = (1 - 2 * (jnp.arange(NK, dtype=jnp.int32) % 2)).astype(jnp.float32)

    def inverse_one(inputs):
        dense_rows, block_mask, coeffs = inputs
        masked = live_table(block_mask, dense_rows)
        coeff_f = coeffs.astype(jnp.float32)
        stacked = jnp.stack([coeff_f, coeff_f * parity], axis=0)
        return jnp.einsum('kj,hrfk->hrfj', masked, stacked).astype(jnp.bfloat16)
    fourier = lax.map(inverse_one, (legendre, pattern, spec_in))
    rows_first = jnp.moveaxis(fourier, 4, 0)
    mixing_f = mixing.astype(jnp.float32)
    synth_scale = (2.0 * MW) ** (-0.5)

    def row_one(inputs):
        fourier_row, row_id = inputs
        length = circle_lengths[row_id]
        cosine_table, sine_table = circle_tables(deal_list, length)
        phases_table = jnp.concatenate([cosine_table, -sine_table], axis=0).astype(jnp.float32)
        coeffs = jnp.transpose(fourier_row, (1, 3, 2, 0)).reshape(2 * FIELDS, 2 * MW).astype(jnp.float32)
        grid_values = (jnp.dot(coeffs, phases_table) * synth_scale).astype(jnp.bfloat16)
        grid_f = grid_values.astype(jnp.float32).reshape(2, FIELDS, -1)
        mixed_sum = jnp.einsum('fg,hgl->hfl', mixing_f, grid_f)
        column = (grid_f + jnp.tanh(mixed_sum)).astype(jnp.bfloat16).reshape(2 * FIELDS, -1)
        weight = jnp.sin(math.pi * (row_id.astype(jnp.float32) + 0.5) / NLAT) / jnp.sqrt(length.astype(jnp.float32))
        analysis = (jnp.dot(column.astype(jnp.float32), phases_table.T) * weight).astype(jnp.bfloat16)
        return jnp.transpose(analysis.reshape(2, FIELDS, 2, MW), (3, 0, 2, 1))
    analysed = lax.map(row_one, (rows_first, jnp.arange(HLAT, dtype=jnp.int32)))
    analysed = jnp.moveaxis(analysed, 0, 4)

    def direct_one(inputs):
        dense_rows, block_mask, coeffs = inputs
        masked = live_table(block_mask, dense_rows)
        product = jnp.einsum('kj,hrfj->hrfk', masked, coeffs.astype(jnp.float32))
        return product[0] + parity * product[1]
    return lax.map(direct_one, (legendre, pattern, analysed))
```

```python
import functools
import math

import jax
import jax.numpy as jnp
from jax import lax
from jax.experimental import pallas as pl
from jax.experimental.pallas import tpu as pltpu
from jax.sharding import PartitionSpec as P

BLK = 128
TILES = 4


def row_kernel(
    fields, lengths, values_ref, mixer_ref, keep_ref, fold_ref, signs_ref, table_ref, weight_ref,
    out_ref, left, total,
):
    rows, lanes = values_ref.shape
    hf = 2 * fields
    width = signs_ref.shape[1]
    waves = width // 2
    span = TILES * BLK
    values = values_ref[...]
    mixed = jnp.concatenate(
        [
            jnp.dot(values[:, at : at + BLK], mixer_ref[...], preferred_element_type=jnp.float32)
            for at in range(0, lanes, BLK)
        ],
        axis=1,
    )
    keep = keep_ref[...]
    scale = (2.0 * waves) ** (-0.5)
    for part, source in enumerate((values.astype(jnp.float32), mixed)):
        spread = (source[:, None, :] * keep[None, :, :]).reshape(rows * hf, lanes)
        folded = scale * jnp.dot(
            spread.astype(jnp.bfloat16), fold_ref[...], preferred_element_type=jnp.float32
        )
        for image in range(4):
            signed = folded * signs_ref[image : image + 1, :]
            at = (2 * image + part) * hf
            left[:, at : at + hf, :] = signed.reshape(rows, hf, width).astype(jnp.bfloat16)

    lane = lax.broadcasted_iota(jnp.int32, (1, span), 1)

    def row_body(row, carry):
        quarter = lengths[row] // 4
        coeffs = left[row]
        step_cos = table_ref[row, 2 * waves : 3 * waves, :]
        step_sin = table_ref[row, 3 * waves : 4 * waves, :]

        def chunk(index, state):
            cos_now, sin_now, sums = state
            cosines, sines = [], []
            for _ in range(TILES):
                cosines.append(cos_now)
                sines.append(-sin_now)
                cos_now, sin_now = (
                    cos_now * step_cos - sin_now * step_sin,
                    sin_now * step_cos + cos_now * step_sin,
                )
            phases = jnp.concatenate(
                [jnp.concatenate(cosines, axis=1), jnp.concatenate(sines, axis=1)], axis=0
            ).astype(jnp.bfloat16)
            grid = jnp.dot(coeffs, phases, preferred_element_type=jnp.float32)
            position = lane + index * span
            share = jnp.where(
                (position == 0) | (position == quarter),
                0.5,
                jnp.where(position < quarter, 1.0, 0.0),
            ).astype(jnp.float32)
            columns = []
            for image in range(4):
                at = 2 * image * hf
                columns.append(
                    ((grid[at : at + hf] + jnp.tanh(grid[at + hf : at + 2 * hf])) * share).astype(
                        jnp.bfloat16
                    )
                )
            sums = sums + lax.dot_general(
                jnp.concatenate(columns, axis=0),
                phases,
                (((1,), (1,)), ((), ())),
                preferred_element_type=jnp.float32,
            )
            return cos_now, sin_now, sums

        start = (
            table_ref[row, 0:waves, :],
            table_ref[row, waves : 2 * waves, :],
            jnp.zeros((4 * hf, width), jnp.float32),
        )
        _, _, sums = lax.fori_loop(0, quarter // span + 1, chunk, start)
        whole = sum(
            sums[image * hf : (image + 1) * hf] * signs_ref[image : image + 1, :]
            for image in range(4)
        )
        total[row] = whole * weight_ref[row]
        return carry

    lax.fori_loop(0, rows, row_body, 0)
    spread = lax.dot_general(
        total[...].reshape(rows * hf, width).astype(jnp.bfloat16),
        fold_ref[...],
        (((1,), (1,)), ((), ())),
        preferred_element_type=jnp.float32,
    )
    out_ref[...] = jnp.sum(spread.reshape(rows, hf, lanes) * keep[None, :, :], axis=1).astype(
        jnp.bfloat16
    )


def wave_tables(deal_list, lengths):
    rows, waves = lengths.shape[0], deal_list.shape[0]
    length = lengths.astype(jnp.float32)[:, None, None]
    wave = deal_list.astype(jnp.float32)[None, :, None]

    def angle_of(position):
        product = wave * position
        turned = product - jnp.floor(product / length) * length
        return turned * (2.0 * math.pi) / length

    inner = angle_of(jnp.arange(BLK, dtype=jnp.float32)[None, None, :])
    step = angle_of(jnp.full((1, 1, 1), float(BLK), jnp.float32))
    shape = (rows, waves, BLK)
    return jnp.concatenate(
        [
            jnp.cos(inner),
            jnp.sin(inner),
            jnp.broadcast_to(jnp.cos(step), shape),
            jnp.broadcast_to(jnp.sin(step), shape),
        ],
        axis=1,
    )


def rows_step(values, row_ids, deal_list, circle_lengths, mixing, slots, half_lat):
    rows, lanes = values.shape
    fields = mixing.shape[0]
    waves = deal_list.shape[0]
    hf, width = 2 * fields, 2 * waves
    lengths = circle_lengths[row_ids]
    tables = wave_tables(deal_list, lengths)
    weight = jnp.sin(math.pi * (row_ids.astype(jnp.float32) + 0.5) / (2 * half_lat)) / jnp.sqrt(
        lengths.astype(jnp.float32)
    )
    weight = jnp.broadcast_to(weight[:, None, None], (rows, 1, width))
    lane = jnp.arange(lanes, dtype=jnp.int32)
    lane_field = lane % fields
    lane_part = lane // fields % 2
    lane_half = lane // (2 * fields) % 2
    lane_wave = lane // (4 * fields)
    keep = (
        (lane_half * fields + lane_field)[None, :] == jnp.arange(hf, dtype=jnp.int32)[:, None]
    ).astype(jnp.float32)
    fold = (
        (lane_part * waves + lane_wave)[:, None] == jnp.arange(width, dtype=jnp.int32)[None, :]
    ).astype(jnp.bfloat16)
    parity = (1 - 2 * (deal_list % 2)).astype(jnp.float32)
    both = jnp.concatenate([parity, parity])
    flip = jnp.concatenate([jnp.ones_like(parity), -jnp.ones_like(parity)])
    signs = jnp.stack([jnp.ones_like(both), flip, both, both * flip])
    block = jnp.arange(BLK, dtype=jnp.int32)
    same = (block[:, None] // fields) == (block[None, :] // fields)
    mixer = jnp.where(
        same, jnp.tile(mixing.T, (BLK // fields, BLK // fields)), jnp.bfloat16(0)
    )
    vmem = pl.BlockSpec(memory_space=pltpu.VMEM)
    return pl.pallas_call(
        functools.partial(row_kernel, fields),
        out_shape=jax.ShapeDtypeStruct((rows, lanes), jnp.bfloat16),
        in_specs=[pl.BlockSpec(memory_space=pltpu.SMEM)] + [vmem] * 7,
        out_specs=vmem,
        scratch_shapes=[
            pltpu.VMEM((rows, 8 * hf, width), jnp.bfloat16),
            pltpu.VMEM((rows, hf, width), jnp.float32),
        ],
    )(lengths, values, mixer, keep, fold, signs, tables, weight)


def local(spec_in, legendre, pattern, deal_list, circle_lengths, mixing):
    lat_index = lax.axis_index("lat")
    lev_index = lax.axis_index("lev")
    lat_count = lax.axis_size("lat")
    lev_count = lax.axis_size("lev")
    slots, local_cols, half_lat = legendre.shape
    fields = spec_in.shape[2]
    devices = lat_count * lev_count
    rows = half_lat // devices
    span = 4 * slots * fields
    global_cols = lev_index * local_cols + jnp.arange(local_cols, dtype=jnp.int32)
    parity = (1 - 2 * (global_cols % 2)).astype(jnp.float32)
    col_live = pattern[:, -1, :][:, global_cols // BLK]
    row_live = jnp.repeat(pattern[:, :, 0], BLK, axis=1)
    kept = spec_in * col_live[:, None, None, :].astype(jnp.bfloat16)
    signed = (kept.astype(jnp.float32) * parity).astype(jnp.bfloat16)
    stacked = jnp.stack([kept, signed], axis=1)
    partial_value = jnp.einsum(
        "skj,shrfk->shrfj", legendre, stacked, preferred_element_type=jnp.float32
    )
    partial_value = partial_value * row_live[:, None, None, None, :].astype(jnp.float32)
    by_device = jnp.transpose(
        partial_value.reshape(span, rows, lev_count, lat_count), (2, 3, 1, 0)
    )
    summed = lax.psum_scatter(by_device, "lev", scatter_dimension=0, tiled=True).astype(
        jnp.bfloat16
    )
    fourier = lax.all_to_all(summed[0], "lat", split_axis=0, concat_axis=0, tiled=True)
    values = jnp.transpose(fourier, (1, 0, 2)).reshape(rows, lat_count * span)
    row_ids = (
        jnp.arange(rows, dtype=jnp.int32) * devices + lev_index * lat_count + lat_index
    )
    analysed = rows_step(values, row_ids, deal_list, circle_lengths, mixing, slots, half_lat)
    leaving = jnp.transpose(analysed.reshape(rows, lat_count, span), (1, 0, 2))
    returned = lax.all_to_all(leaving, "lat", split_axis=0, concat_axis=0, tiled=True)
    gathered = lax.all_gather(returned, "lev", axis=0, tiled=False)
    ordered = jnp.transpose(gathered, (3, 2, 0, 1)).reshape(slots, 2, 2, fields, half_lat)
    ordered = ordered * row_live[:, None, None, None, :].astype(jnp.bfloat16)
    product = jnp.einsum(
        "skj,shrfj->shrfk", legendre, ordered, preferred_element_type=jnp.float32
    )
    live = col_live[:, None, None, :].astype(jnp.float32)
    return (product[:, 0] + parity * product[:, 1]) * live


def solution(mesh):
    return jax.shard_map(
        local,
        mesh=mesh,
        in_specs=(
            P("lat", None, None, "lev"),
            P("lat", "lev", None),
            P("lat", None, None),
            P(),
            P(),
            P(),
        ),
        out_specs=P("lat", None, None, "lev"),
        check_vma=False,
    )
```

```python
import functools
import math

import jax
import jax.numpy as jnp
from jax import lax
from jax.experimental import pallas as pl
from jax.experimental.pallas import tpu as pltpu
from jax.sharding import PartitionSpec as P

BLK = 128
TILES = 4


def row_kernel(
    fields, lengths, values_ref, live_ref, mixer_ref, keep_ref, fold_ref, signs_ref, table_ref, weight_ref,
    out_ref, left, total,
):
    rows, lanes = values_ref.shape
    hf = 2 * fields
    width = signs_ref.shape[1]
    waves = width // 2
    span = TILES * BLK
    live = live_ref[...]
    values = values_ref[...] * live
    mixed = jnp.concatenate(
        [
            jnp.dot(values[:, at : at + BLK], mixer_ref[...], preferred_element_type=jnp.float32)
            for at in range(0, lanes, BLK)
        ],
        axis=1,
    )
    keep = keep_ref[...]
    scale = (2.0 * waves) ** (-0.5)
    for part, source in enumerate((values.astype(jnp.float32), mixed)):
        spread = (source[:, None, :] * keep[None, :, :]).reshape(rows * hf, lanes)
        folded = scale * jnp.dot(
            spread.astype(jnp.bfloat16), fold_ref[...], preferred_element_type=jnp.float32
        )
        for image in range(4):
            signed = folded * signs_ref[image : image + 1, :]
            at = (2 * image + part) * hf
            left[:, at : at + hf, :] = signed.reshape(rows, hf, width).astype(jnp.bfloat16)

    lane = lax.broadcasted_iota(jnp.int32, (1, span), 1)

    def row_body(row, carry):
        quarter = lengths[row] // 4
        coeffs = left[row]
        step_cos = table_ref[row, 2 * waves : 3 * waves, :]
        step_sin = table_ref[row, 3 * waves : 4 * waves, :]

        def chunk(index, state):
            cos_now, sin_now, sums = state
            cosines, sines = [], []
            for _ in range(TILES):
                cosines.append(cos_now)
                sines.append(-sin_now)
                cos_now, sin_now = (
                    cos_now * step_cos - sin_now * step_sin,
                    sin_now * step_cos + cos_now * step_sin,
                )
            phases = jnp.concatenate(
                [jnp.concatenate(cosines, axis=1), jnp.concatenate(sines, axis=1)], axis=0
            ).astype(jnp.bfloat16)
            grid = jnp.dot(coeffs, phases, preferred_element_type=jnp.float32)
            position = lane + index * span
            share = jnp.where(
                (position == 0) | (position == quarter),
                0.5,
                jnp.where(position < quarter, 1.0, 0.0),
            ).astype(jnp.float32)
            columns = []
            for image in range(4):
                at = 2 * image * hf
                columns.append(
                    ((grid[at : at + hf] + jnp.tanh(grid[at + hf : at + 2 * hf])) * share).astype(
                        jnp.bfloat16
                    )
                )
            sums = sums + lax.dot_general(
                jnp.concatenate(columns, axis=0),
                phases,
                (((1,), (1,)), ((), ())),
                preferred_element_type=jnp.float32,
            )
            return cos_now, sin_now, sums

        start = (
            table_ref[row, 0:waves, :],
            table_ref[row, waves : 2 * waves, :],
            jnp.zeros((4 * hf, width), jnp.float32),
        )
        _, _, sums = lax.fori_loop(0, quarter // span + 1, chunk, start)
        whole = sum(
            sums[image * hf : (image + 1) * hf] * signs_ref[image : image + 1, :]
            for image in range(4)
        )
        total[row] = whole * weight_ref[row]
        return carry

    lax.fori_loop(0, rows, row_body, 0)
    spread = lax.dot_general(
        total[...].reshape(rows * hf, width).astype(jnp.bfloat16),
        fold_ref[...],
        (((1,), (1,)), ((), ())),
        preferred_element_type=jnp.float32,
    )
    summed = jnp.sum(spread.reshape(rows, hf, lanes) * keep[None, :, :], axis=1)
    out_ref[...] = summed.astype(jnp.bfloat16) * live


def wave_tables(deal_list, lengths):
    rows, waves = lengths.shape[0], deal_list.shape[0]
    length = lengths.astype(jnp.float32)[:, None, None]
    wave = deal_list.astype(jnp.float32)[None, :, None]

    def angle_of(position):
        product = wave * position
        turned = product - jnp.floor(product / length) * length
        return turned * (2.0 * math.pi) / length

    inner = angle_of(jnp.arange(BLK, dtype=jnp.float32)[None, None, :])
    step = angle_of(jnp.full((1, 1, 1), float(BLK), jnp.float32))
    shape = (rows, waves, BLK)
    return jnp.concatenate(
        [
            jnp.cos(inner),
            jnp.sin(inner),
            jnp.broadcast_to(jnp.cos(step), shape),
            jnp.broadcast_to(jnp.sin(step), shape),
        ],
        axis=1,
    )


def rows_step(values, row_ids, deal_list, circle_lengths, mixing, slots, half_lat):
    rows, lanes = values.shape
    fields = mixing.shape[0]
    waves = deal_list.shape[0]
    hf, width = 2 * fields, 2 * waves
    lengths = circle_lengths[row_ids]
    tables = wave_tables(deal_list, lengths)
    weight = jnp.sin(math.pi * (row_ids.astype(jnp.float32) + 0.5) / (2 * half_lat)) / jnp.sqrt(
        lengths.astype(jnp.float32)
    )
    weight = jnp.broadcast_to(weight[:, None, None], (rows, 1, width))
    lane = jnp.arange(lanes, dtype=jnp.int32)
    lane_field = lane % fields
    lane_part = lane // fields % 2
    lane_half = lane // (2 * fields) % 2
    lane_wave = lane // (4 * fields)
    first_live = (deal_list * (half_lat // BLK)) // (2 * half_lat)
    first_lane = jnp.repeat(first_live, lanes // waves)
    live = (row_ids[:, None] // BLK >= first_lane[None, :]).astype(jnp.bfloat16)
    keep = (
        (lane_half * fields + lane_field)[None, :] == jnp.arange(hf, dtype=jnp.int32)[:, None]
    ).astype(jnp.float32)
    fold = (
        (lane_part * waves + lane_wave)[:, None] == jnp.arange(width, dtype=jnp.int32)[None, :]
    ).astype(jnp.bfloat16)
    parity = (1 - 2 * (deal_list % 2)).astype(jnp.float32)
    both = jnp.concatenate([parity, parity])
    flip = jnp.concatenate([jnp.ones_like(parity), -jnp.ones_like(parity)])
    signs = jnp.stack([jnp.ones_like(both), flip, both, both * flip])
    block = jnp.arange(BLK, dtype=jnp.int32)
    same = (block[:, None] // fields) == (block[None, :] // fields)
    mixer = jnp.where(
        same, jnp.tile(mixing.T, (BLK // fields, BLK // fields)), jnp.bfloat16(0)
    )
    vmem = pl.BlockSpec(memory_space=pltpu.VMEM)
    return pl.pallas_call(
        functools.partial(row_kernel, fields),
        out_shape=jax.ShapeDtypeStruct((rows, lanes), jnp.bfloat16),
        in_specs=[pl.BlockSpec(memory_space=pltpu.SMEM)] + [vmem] * 8,
        out_specs=vmem,
        scratch_shapes=[
            pltpu.VMEM((rows, 8 * hf, width), jnp.bfloat16),
            pltpu.VMEM((rows, hf, width), jnp.float32),
        ],
    )(lengths, values, live, mixer, keep, fold, signs, tables, weight)


def peers_of(axis):
    count = lax.axis_size(axis)
    return [lax.rem(lax.axis_index(axis) + off, count) for off in range(1, count)]


def greet():
    barrier = pltpu.get_barrier_semaphore()
    total = 0
    for axis in ("lat", "lev"):
        for peer in peers_of(axis):
            pl.semaphore_signal(
                barrier, inc=1, device_id={axis: peer}, device_id_type=pl.DeviceIdType.MESH
            )
            total += 1
    pl.semaphore_wait(barrier, total)


def send(axis, sources, target, sems):
    copies = []
    for step, peer in enumerate(peers_of(axis)):
        copy = pltpu.make_async_remote_copy(
            src_ref=sources(peer),
            dst_ref=target,
            send_sem=sems.at[0, step],
            recv_sem=sems.at[1, step],
            device_id={axis: peer},
            device_id_type=pl.DeviceIdType.MESH,
        )
        copy.start()
        copies.append(copy)
    return copies


def inward_kernel(pack, spec_ref, legendre_ref, out_ref, turned, leaving, arriving, summed, landed,
                  lev_sems, lat_sems):
    slots, _, half_lat = legendre_ref.shape
    lev_count, lat_count, count, width = leaving.shape
    devices = lev_count * lat_count
    lev_index, lat_index = lax.axis_index("lev"), lax.axis_index("lat")
    packed = half_lat // pack
    sums = [
        jnp.dot(spec_ref[slot], legendre_ref[slot], preferred_element_type=jnp.float32)
        for slot in range(slots)
    ]
    for block in range(packed // BLK):
        piece = jnp.concatenate(
            [
                value[:, part * packed + block * BLK : part * packed + (block + 1) * BLK]
                for part in range(pack)
                for value in sums
            ],
            axis=0,
        )
        turned[:, block * BLK : (block + 1) * BLK, :] = jnp.stack(
            [piece[at : at + BLK].T for at in range(0, width, BLK)]
        )
    for device in range(devices):
        for at in range(width // BLK):
            leaving[device // lat_count, device % lat_count, :, at * BLK : (at + 1) * BLK] = (
                turned[at, pl.ds(device, count, stride=devices), :].astype(jnp.bfloat16)
            )
    greet()
    copies = send("lev", lambda peer: leaving.at[peer], arriving.at[lev_index], lev_sems)
    total = leaving[lev_index].astype(jnp.float32)
    for copy, peer in zip(copies, [lax.rem(lev_index + lev_count - off, lev_count) for off in range(1, lev_count)]):
        copy.wait_recv()
        total = total + arriving[peer].astype(jnp.float32)
    summed[...] = total.astype(jnp.bfloat16)
    crossing = send("lat", lambda peer: summed.at[peer], landed.at[lat_index], lat_sems)
    out_ref[lat_index] = summed[lat_index]
    for copy, peer in zip(crossing, [lax.rem(lat_index + lat_count - off, lat_count) for off in range(1, lat_count)]):
        copy.wait_recv()
        out_ref[peer] = landed[peer]
    for copy in copies + crossing:
        copy.wait_send()


def outward_kernel(pack, fields, rows_ref, legendre_ref, out_ref, held, landed, gathered, turned,
                   lev_sems, lat_sems, load_sem):
    slots, local_cols, half_lat = held.shape
    lev_count, lat_count, count, width = gathered.shape
    devices = lev_count * lat_count
    lev_index, lat_index = lax.axis_index("lev"), lax.axis_index("lat")
    packed = half_lat // pack
    part_width = 4 * fields
    load = pltpu.make_async_copy(legendre_ref, held, load_sem)
    load.start()
    greet()
    crossing = send("lat", lambda peer: rows_ref.at[peer], landed.at[lat_index], lat_sems)
    landed[lat_index] = rows_ref[lat_index]
    for copy in crossing:
        copy.wait_recv()
    copies = send("lev", lambda peer: landed, gathered.at[lev_index], lev_sems)
    gathered[lev_index] = landed[...]
    for copy in copies:
        copy.wait_recv()
    for device in range(devices):
        block = gathered[device // lat_count, device % lat_count].astype(jnp.float32)
        for at in range(width // BLK):
            turned[at, pl.ds(device, count, stride=devices), :] = block[:, at * BLK : (at + 1) * BLK]
    load.wait()
    sides = [turned[at].astype(jnp.bfloat16) for at in range(width // BLK)]
    for slot in range(slots):
        total = None
        for part in range(pack):
            at = part * slots * part_width + slot * part_width
            value = jnp.dot(
                held[slot, :, part * packed : (part + 1) * packed],
                sides[at // BLK],
                preferred_element_type=jnp.float32,
            )[:, at % BLK : at % BLK + part_width]
            total = value if total is None else total + value
        out_ref[slot] = total
    for copy in copies + crossing:
        copy.wait_send()


def local(spec_in, legendre, pattern, deal_list, circle_lengths, mixing):
    lat_index = lax.axis_index("lat")
    lev_index = lax.axis_index("lev")
    lat_count = lax.axis_size("lat")
    lev_count = lax.axis_size("lev")
    slots, local_cols, half_lat = legendre.shape
    fields = spec_in.shape[2]
    devices = lat_count * lev_count
    rows = half_lat // devices
    span = 4 * slots * fields
    pack = max(1, BLK // span)
    count, width = rows // pack, span * pack
    global_cols = lev_index * local_cols + jnp.arange(local_cols, dtype=jnp.int32)
    parity = (1 - 2 * (global_cols % 2)).astype(jnp.float32)
    chooser = (
        global_cols[None, :] // BLK
        == jnp.arange(pattern.shape[2], dtype=jnp.int32)[:, None]
    )
    col_live = jnp.sum(
        jnp.where(chooser[None], pattern[:, -1, :, None], 0), axis=1
    ).astype(jnp.float32)
    kept = spec_in.astype(jnp.float32) * col_live[:, None, None, :]
    stacked = (
        jnp.stack([kept, kept * parity], axis=1)
        .astype(jnp.bfloat16)
        .reshape(slots, 4 * fields, local_cols)
    )
    vmem = pl.BlockSpec(memory_space=pltpu.VMEM)
    block_shape = (lat_count, count, width)
    sems = [
        pltpu.SemaphoreType.DMA((2, lev_count)),
        pltpu.SemaphoreType.DMA((2, lat_count)),
    ]
    turned = pltpu.VMEM((width // BLK, half_lat // pack, BLK), jnp.float32)
    fourier = pl.pallas_call(
        functools.partial(inward_kernel, pack),
        out_shape=jax.ShapeDtypeStruct(block_shape, jnp.bfloat16),
        in_specs=[vmem, vmem],
        out_specs=vmem,
        scratch_shapes=[
            turned,
            pltpu.VMEM((lev_count,) + block_shape, jnp.bfloat16),
            pltpu.VMEM((lev_count,) + block_shape, jnp.bfloat16),
            pltpu.VMEM(block_shape, jnp.bfloat16),
            pltpu.VMEM(block_shape, jnp.bfloat16),
        ]
        + sems,
        compiler_params=pltpu.CompilerParams(collective_id=0, has_side_effects=True),
    )(stacked, legendre)
    values = jnp.transpose(
        fourier.reshape(lat_count, count, pack, span), (2, 1, 0, 3)
    ).reshape(rows, lat_count * span)
    row_ids = (
        jnp.arange(pack, dtype=jnp.int32)[:, None] * (half_lat // pack)
        + jnp.arange(count, dtype=jnp.int32)[None, :] * devices
        + (lev_index * lat_count + lat_index)
    ).reshape(rows)
    analysed = rows_step(values, row_ids, deal_list, circle_lengths, mixing, slots, half_lat)
    leaving = jnp.transpose(
        analysed.reshape(pack, count, lat_count, span), (2, 1, 0, 3)
    ).reshape(block_shape)
    product = pl.pallas_call(
        functools.partial(outward_kernel, pack, fields),
        out_shape=jax.ShapeDtypeStruct((slots, local_cols, 4 * fields), jnp.float32),
        in_specs=[vmem, pl.BlockSpec(memory_space=pl.ANY)],
        out_specs=vmem,
        scratch_shapes=[
            pltpu.VMEM(legendre.shape, jnp.bfloat16),
            pltpu.VMEM(block_shape, jnp.bfloat16),
            pltpu.VMEM((lev_count,) + block_shape, jnp.bfloat16),
            turned,
        ]
        + sems
        + [pltpu.SemaphoreType.DMA],
        compiler_params=pltpu.CompilerParams(collective_id=1, has_side_effects=True),
    )(leaving, legendre)
    product = jnp.transpose(product, (0, 2, 1)).reshape(slots, 2, 2, fields, local_cols)
    return (product[:, 0] + parity * product[:, 1]) * col_live[:, None, None, :]


def solution(mesh):
    return jax.shard_map(
        local,
        mesh=mesh,
        in_specs=(
            P("lat", None, None, "lev"),
            P("lat", "lev", None),
            P("lat", None, None),
            P(),
            P(),
            P(),
        ),
        out_specs=P("lat", None, None, "lev"),
        check_vma=False,
    )
```

```python
import functools
import math

import jax
import jax.numpy as jnp
from jax import lax
from jax.experimental import pallas as pl
from jax.experimental.pallas import tpu as pltpu
from jax.sharding import PartitionSpec as P

BLK = 128
TILES = 2
STREAMS = 8


def row_kernel(
    fields, lengths, values_ref, live_ref, mixer_ref, keep_ref, fold_ref, signs_ref, table_ref, weight_ref,
    out_ref, left, total,
):
    rows, lanes = values_ref.shape
    hf = 2 * fields
    width = signs_ref.shape[1]
    waves = width // 2
    span = TILES * BLK
    live = live_ref[...]
    values = values_ref[...] * live
    mixed = jnp.concatenate(
        [
            jnp.dot(values[:, at : at + BLK], mixer_ref[...], preferred_element_type=jnp.float32)
            for at in range(0, lanes, BLK)
        ],
        axis=1,
    )
    keep = keep_ref[...]
    scale = (2.0 * waves) ** (-0.5)

    def fold(source):
        spread = (source[:, None, :] * keep[None, :, :]).reshape(rows * hf, lanes)
        return scale * jnp.dot(
            spread.astype(jnp.bfloat16), fold_ref[...], preferred_element_type=jnp.float32
        )

    high = mixed.astype(jnp.bfloat16).astype(jnp.float32)
    straight, mix_high, mix_low = fold(values.astype(jnp.float32)), fold(high), fold(mixed - high)
    pairs = (
        jnp.concatenate([straight, jnp.zeros_like(straight)], axis=1),
        jnp.concatenate([mix_high, mix_low], axis=1),
    )
    for part, source in enumerate(pairs):
        for image in range(4):
            sign = signs_ref[image : image + 1, :]
            signed = source * jnp.concatenate([sign, sign], axis=1)
            at = (2 * image + part) * hf
            left[:rows, at : at + hf, :] = signed.reshape(rows, hf, 2 * width).astype(jnp.bfloat16)

    lane = lax.broadcasted_iota(jnp.int32, (1, span), 1)

    def proceed(state):
        return state[1]

    def advance(state):
        following, _, streams = state
        stages = []
        for row, index, cos_held, sin_held, sums in streams:
            quarter = lengths[jnp.minimum(row, rows - 1)] // 4
            at = jnp.minimum(row, rows - 1)
            fresh = index == 0
            cos_now = jnp.where(fresh, table_ref[at, 0:waves, :], cos_held)
            sin_now = jnp.where(fresh, table_ref[at, waves : 2 * waves, :], sin_held)
            step_cos = table_ref[at, 2 * waves : 3 * waves, :]
            step_sin = table_ref[at, 3 * waves : 4 * waves, :]
            cosines, sines = [], []
            for _ in range(TILES):
                cosines.append(cos_now)
                sines.append(-sin_now)
                cos_now, sin_now = (
                    cos_now * step_cos - sin_now * step_sin,
                    sin_now * step_cos + cos_now * step_sin,
                )
            phases = jnp.concatenate(
                [jnp.concatenate(cosines, axis=1), jnp.concatenate(sines, axis=1)], axis=0
            ).astype(jnp.bfloat16)
            stages.append((at, quarter, fresh, cos_now, sin_now, phases))
        grids = [
            jnp.dot(
                left[stage[0]],
                jnp.concatenate([stage[5], stage[5]], axis=0),
                preferred_element_type=jnp.float32,
            )
            for stage in stages
        ]
        added = []
        for stream, stage, grid in zip(streams, stages, grids):
            quarter, phases = stage[1], stage[5]
            position = lane + stream[1] * span
            share = jnp.where(
                (position == 0) | (position == quarter),
                0.5,
                jnp.where(position < quarter, 1.0, 0.0),
            ).astype(jnp.float32)
            columns = []
            for image in range(4):
                at = 2 * image * hf
                columns.append(
                    ((grid[at : at + hf] + jnp.tanh(grid[at + hf : at + 2 * hf])) * share).astype(
                        jnp.bfloat16
                    )
                )
            added.append(
                lax.dot_general(
                    jnp.concatenate(columns, axis=0),
                    phases,
                    (((1,), (1,)), ((), ())),
                    preferred_element_type=jnp.float32,
                )
            )
        later = []
        busy = jnp.bool_(False)
        for stream, stage, extra in zip(streams, stages, added):
            row, index, _, _, sums = stream
            sums = jnp.where(stage[2], 0.0, sums) + extra
            whole = sum(
                sums[image * hf : (image + 1) * hf] * signs_ref[image : image + 1, :]
                for image in range(4)
            )
            total[row] = whole * weight_ref[stage[0]]
            done = (index + 1) * span > stage[1]
            idle = row >= rows
            taken = jnp.logical_and(done, jnp.logical_not(idle))
            row = jnp.where(taken, following, row)
            following = following - taken.astype(jnp.int32)
            row = jnp.where(row < 0, rows, row)
            index = jnp.where(done, 0, index + 1)
            busy = jnp.logical_or(busy, row < rows)
            later.append((row, index, stage[3], stage[4], sums))
        return following, busy, tuple(later)

    held = jnp.zeros((waves, BLK), jnp.float32)
    streams = tuple(
        (
            jnp.int32(rows - 1 - stream if stream < rows else rows),
            jnp.int32(0),
            held,
            held,
            jnp.zeros((4 * hf, width), jnp.float32),
        )
        for stream in range(STREAMS)
    )
    lax.while_loop(
        proceed, advance, (jnp.int32(rows - 1 - STREAMS), jnp.bool_(True), streams)
    )
    spread = lax.dot_general(
        total[:rows].reshape(rows * hf, width).astype(jnp.bfloat16),
        fold_ref[...],
        (((1,), (1,)), ((), ())),
        preferred_element_type=jnp.float32,
    )
    summed = jnp.sum(spread.reshape(rows, hf, lanes) * keep[None, :, :], axis=1)
    out_ref[...] = summed.astype(jnp.bfloat16) * live


def wave_tables(deal_list, lengths):
    rows, waves = lengths.shape[0], deal_list.shape[0]
    length = lengths.astype(jnp.float32)[:, None, None]
    wave = deal_list.astype(jnp.float32)[None, :, None]

    def angle_of(position):
        product = wave * position
        turned = product - jnp.floor(product / length) * length
        return turned * (2.0 * math.pi) / length

    inner = angle_of(jnp.arange(BLK, dtype=jnp.float32)[None, None, :])
    step = angle_of(jnp.full((1, 1, 1), float(BLK), jnp.float32))
    shape = (rows, waves, BLK)
    return jnp.concatenate(
        [
            jnp.cos(inner),
            jnp.sin(inner),
            jnp.broadcast_to(jnp.cos(step), shape),
            jnp.broadcast_to(jnp.sin(step), shape),
        ],
        axis=1,
    )


def rows_step(values, row_ids, deal_list, circle_lengths, mixing, slots, half_lat):
    rows, lanes = values.shape
    fields = mixing.shape[0]
    waves = deal_list.shape[0]
    hf, width = 2 * fields, 2 * waves
    lengths = circle_lengths[row_ids]
    tables = wave_tables(deal_list, lengths)
    weight = jnp.sin(math.pi * (row_ids.astype(jnp.float32) + 0.5) / (2 * half_lat)) / jnp.sqrt(
        lengths.astype(jnp.float32)
    )
    weight = jnp.broadcast_to(weight[:, None, None], (rows, 1, width))
    lane = jnp.arange(lanes, dtype=jnp.int32)
    lane_field = lane % fields
    lane_part = lane // fields % 2
    lane_half = lane // (2 * fields) % 2
    lane_wave = lane // (4 * fields)
    first_live = (deal_list * (half_lat // BLK)) // (2 * half_lat)
    first_lane = jnp.repeat(first_live, lanes // waves)
    live = (row_ids[:, None] // BLK >= first_lane[None, :]).astype(jnp.bfloat16)
    keep = (
        (lane_half * fields + lane_field)[None, :] == jnp.arange(hf, dtype=jnp.int32)[:, None]
    ).astype(jnp.float32)
    fold = (
        (lane_part * waves + lane_wave)[:, None] == jnp.arange(width, dtype=jnp.int32)[None, :]
    ).astype(jnp.bfloat16)
    parity = (1 - 2 * (deal_list % 2)).astype(jnp.float32)
    both = jnp.concatenate([parity, parity])
    flip = jnp.concatenate([jnp.ones_like(parity), -jnp.ones_like(parity)])
    signs = jnp.stack([jnp.ones_like(both), flip, both, both * flip])
    block = jnp.arange(BLK, dtype=jnp.int32)
    same = (block[:, None] // fields) == (block[None, :] // fields)
    mixer = jnp.where(
        same, jnp.tile(mixing.T, (BLK // fields, BLK // fields)), jnp.bfloat16(0)
    )
    vmem = pl.BlockSpec(memory_space=pltpu.VMEM)
    return pl.pallas_call(
        functools.partial(row_kernel, fields),
        out_shape=jax.ShapeDtypeStruct((rows, lanes), jnp.bfloat16),
        in_specs=[pl.BlockSpec(memory_space=pltpu.SMEM)] + [vmem] * 8,
        out_specs=vmem,
        scratch_shapes=[
            pltpu.VMEM((rows, 8 * hf, 2 * width), jnp.bfloat16),
            pltpu.VMEM((rows + 1, hf, width), jnp.float32),
        ],
    )(lengths, values, live, mixer, keep, fold, signs, tables, weight)


def peers_of(axis):
    count = lax.axis_size(axis)
    return [lax.rem(lax.axis_index(axis) + off, count) for off in range(1, count)]


def greet():
    barrier = pltpu.get_barrier_semaphore()
    total = 0
    for axis in ("lat", "lev"):
        for peer in peers_of(axis):
            pl.semaphore_signal(
                barrier, inc=1, device_id={axis: peer}, device_id_type=pl.DeviceIdType.MESH
            )
            total += 1
    pl.semaphore_wait(barrier, total)


def send(axis, sources, target, sems):
    copies = []
    for step, peer in enumerate(peers_of(axis)):
        copy = pltpu.make_async_remote_copy(
            src_ref=sources(peer),
            dst_ref=target,
            send_sem=sems.at[0, step],
            recv_sem=sems.at[1, step],
            device_id={axis: peer},
            device_id_type=pl.DeviceIdType.MESH,
        )
        copy.start()
        copies.append(copy)
    return copies


def inward_kernel(pack, spec_ref, legendre_ref, out_ref, turned, leaving, arriving, summed, landed,
                  lev_sems, lat_sems):
    slots, _, half_lat = legendre_ref.shape
    lev_count, lat_count, count, width = leaving.shape
    devices = lev_count * lat_count
    lev_index, lat_index = lax.axis_index("lev"), lax.axis_index("lat")
    packed = half_lat // pack
    sums = [
        jnp.dot(spec_ref[slot], legendre_ref[slot], preferred_element_type=jnp.float32)
        for slot in range(slots)
    ]
    for block in range(packed // BLK):
        piece = jnp.concatenate(
            [
                value[:, part * packed + block * BLK : part * packed + (block + 1) * BLK]
                for part in range(pack)
                for value in sums
            ],
            axis=0,
        )
        turned[:, block * BLK : (block + 1) * BLK, :] = jnp.stack(
            [piece[at : at + BLK].T for at in range(0, width, BLK)]
        )
    for device in range(devices):
        for at in range(width // BLK):
            leaving[device // lat_count, device % lat_count, :, at * BLK : (at + 1) * BLK] = (
                turned[at, pl.ds(device, count, stride=devices), :].astype(jnp.bfloat16)
            )
    greet()
    copies = send("lev", lambda peer: leaving.at[peer], arriving.at[lev_index], lev_sems)
    mine = lev_index * lat_count
    total = jnp.stack(
        [
            jnp.concatenate(
                [
                    turned[at, pl.ds(mine + side, count, stride=devices), :]
                    for at in range(width // BLK)
                ],
                axis=1,
            )
            for side in range(lat_count)
        ]
    )
    for copy, peer in zip(copies, [lax.rem(lev_index + lev_count - off, lev_count) for off in range(1, lev_count)]):
        copy.wait_recv()
        total = total + arriving[peer].astype(jnp.float32)
    summed[...] = total.astype(jnp.bfloat16)
    crossing = send("lat", lambda peer: summed.at[peer], landed.at[lat_index], lat_sems)
    out_ref[lat_index] = summed[lat_index]
    for copy, peer in zip(crossing, [lax.rem(lat_index + lat_count - off, lat_count) for off in range(1, lat_count)]):
        copy.wait_recv()
        out_ref[peer] = landed[peer]
    for copy in copies + crossing:
        copy.wait_send()


def outward_kernel(pack, fields, rows_ref, legendre_ref, out_ref, held, landed, gathered, turned,
                   lev_sems, lat_sems, load_sem):
    slots, local_cols, half_lat = held.shape
    lev_count, lat_count, count, width = gathered.shape
    devices = lev_count * lat_count
    lev_index, lat_index = lax.axis_index("lev"), lax.axis_index("lat")
    packed = half_lat // pack
    part_width = 4 * fields
    load = pltpu.make_async_copy(legendre_ref, held, load_sem)
    load.start()
    greet()
    crossing = send("lat", lambda peer: rows_ref.at[peer], landed.at[lat_index], lat_sems)
    landed[lat_index] = rows_ref[lat_index]
    for copy in crossing:
        copy.wait_recv()
    copies = send("lev", lambda peer: landed, gathered.at[lev_index], lev_sems)
    gathered[lev_index] = landed[...]
    for copy in copies:
        copy.wait_recv()
    for device in range(devices):
        block = gathered[device // lat_count, device % lat_count].astype(jnp.float32)
        for at in range(width // BLK):
            turned[at, pl.ds(device, count, stride=devices), :] = block[:, at * BLK : (at + 1) * BLK]
    load.wait()
    sides = [turned[at].astype(jnp.bfloat16) for at in range(width // BLK)]
    for slot in range(slots):
        total = None
        for part in range(pack):
            at = part * slots * part_width + slot * part_width
            value = jnp.dot(
                held[slot, :, part * packed : (part + 1) * packed],
                sides[at // BLK],
                preferred_element_type=jnp.float32,
            )[:, at % BLK : at % BLK + part_width]
            total = value if total is None else total + value
        out_ref[slot] = total
    for copy in copies + crossing:
        copy.wait_send()


def local(spec_in, legendre, pattern, deal_list, circle_lengths, mixing):
    lat_index = lax.axis_index("lat")
    lev_index = lax.axis_index("lev")
    lat_count = lax.axis_size("lat")
    lev_count = lax.axis_size("lev")
    slots, local_cols, half_lat = legendre.shape
    fields = spec_in.shape[2]
    devices = lat_count * lev_count
    rows = half_lat // devices
    span = 4 * slots * fields
    pack = max(1, BLK // span)
    count, width = rows // pack, span * pack
    global_cols = lev_index * local_cols + jnp.arange(local_cols, dtype=jnp.int32)
    parity = (1 - 2 * (global_cols % 2)).astype(jnp.float32)
    chooser = (
        global_cols[None, :] // BLK
        == jnp.arange(pattern.shape[2], dtype=jnp.int32)[:, None]
    )
    col_live = jnp.sum(
        jnp.where(chooser[None], pattern[:, -1, :, None], 0), axis=1
    ).astype(jnp.float32)
    kept = spec_in.astype(jnp.float32) * col_live[:, None, None, :]
    stacked = (
        jnp.stack([kept, kept * parity], axis=1)
        .astype(jnp.bfloat16)
        .reshape(slots, 4 * fields, local_cols)
    )
    vmem = pl.BlockSpec(memory_space=pltpu.VMEM)
    block_shape = (lat_count, count, width)
    sems = [
        pltpu.SemaphoreType.DMA((2, lev_count)),
        pltpu.SemaphoreType.DMA((2, lat_count)),
    ]
    turned = pltpu.VMEM((width // BLK, half_lat // pack, BLK), jnp.float32)
    fourier = pl.pallas_call(
        functools.partial(inward_kernel, pack),
        out_shape=jax.ShapeDtypeStruct(block_shape, jnp.bfloat16),
        in_specs=[vmem, vmem],
        out_specs=vmem,
        scratch_shapes=[
            turned,
            pltpu.VMEM((lev_count,) + block_shape, jnp.bfloat16),
            pltpu.VMEM((lev_count,) + block_shape, jnp.bfloat16),
            pltpu.VMEM(block_shape, jnp.bfloat16),
            pltpu.VMEM(block_shape, jnp.bfloat16),
        ]
        + sems,
        compiler_params=pltpu.CompilerParams(collective_id=0, has_side_effects=True),
    )(stacked, legendre)
    values = jnp.transpose(
        fourier.reshape(lat_count, count, pack, span), (2, 1, 0, 3)
    ).reshape(rows, lat_count * span)
    row_ids = (
        jnp.arange(pack, dtype=jnp.int32)[:, None] * (half_lat // pack)
        + jnp.arange(count, dtype=jnp.int32)[None, :] * devices
        + (lev_index * lat_count + lat_index)
    ).reshape(rows)
    analysed = rows_step(values, row_ids, deal_list, circle_lengths, mixing, slots, half_lat)
    leaving = jnp.transpose(
        analysed.reshape(pack, count, lat_count, span), (2, 1, 0, 3)
    ).reshape(block_shape)
    product = pl.pallas_call(
        functools.partial(outward_kernel, pack, fields),
        out_shape=jax.ShapeDtypeStruct((slots, local_cols, 4 * fields), jnp.float32),
        in_specs=[vmem, pl.BlockSpec(memory_space=pl.ANY)],
        out_specs=vmem,
        scratch_shapes=[
            pltpu.VMEM(legendre.shape, jnp.bfloat16),
            pltpu.VMEM(block_shape, jnp.bfloat16),
            pltpu.VMEM((lev_count,) + block_shape, jnp.bfloat16),
            turned,
        ]
        + sems
        + [pltpu.SemaphoreType.DMA],
        compiler_params=pltpu.CompilerParams(collective_id=1, has_side_effects=True),
    )(leaving, legendre)
    product = jnp.transpose(product, (0, 2, 1)).reshape(slots, 2, 2, fields, local_cols)
    return (product[:, 0] + parity * product[:, 1]) * col_live[:, None, None, :]


def solution(mesh):
    return jax.shard_map(
        local,
        mesh=mesh,
        in_specs=(
            P("lat", None, None, "lev"),
            P("lat", "lev", None),
            P("lat", None, None),
            P(),
            P(),
            P(),
        ),
        out_specs=P("lat", None, None, "lev"),
        check_vma=False,
    )
```

```python
import functools
import math

import jax
import jax.numpy as jnp
from jax import lax
from jax.experimental import pallas as pl
from jax.experimental.pallas import tpu as pltpu
from jax.sharding import PartitionSpec as P

BLK = 128
TILES = 2
STREAMS = 12


def row_kernel(
    packed, lengths, deal, fourier_ref, mixing_ref, table_ref, weight_ref, out_ref, left, total
):
    lat_count, count, block_width = fourier_ref.shape
    rows = table_ref.shape[0]
    waves = table_ref.shape[1] // 4
    fields = mixing_ref.shape[0]
    hf, width = 2 * fields, 2 * waves
    pack = rows // count
    part_span = block_width // pack
    lanes = lat_count * part_span
    span = TILES * BLK
    devices = lat_count * lax.axis_size("lev")
    device = lax.axis_index("lev") * lat_count + lax.axis_index("lat")
    lane_of = lax.broadcasted_iota(jnp.int32, (1, lanes), 1)
    first_lane = jnp.zeros((1, lanes), jnp.int32)
    kind = lax.broadcasted_iota(jnp.int32, (1, width), 1)
    both = jnp.zeros((1, width), jnp.float32)
    for wave in range(waves):
        cut = deal[wave] * (pack * packed // BLK) // (2 * pack * packed)
        first_lane = jnp.where(lane_of // (4 * fields) == wave, cut, first_lane)
        odd = (1 - 2 * (deal[wave] % 2)).astype(jnp.float32)
        both = jnp.where(kind % waves == wave, odd, both)
    flip = jnp.where(kind < waves, 1.0, -1.0).astype(jnp.float32)
    signs = [jnp.ones_like(both), flip, both, both * flip]
    blocks = [fourier_ref[side].astype(jnp.float32) for side in range(lat_count)]
    values = jnp.concatenate(
        [
            jnp.concatenate(
                [block[:, part * part_span : (part + 1) * part_span] for block in blocks], axis=1
            )
            for part in range(pack)
        ],
        axis=0,
    )
    row_in = lax.broadcasted_iota(jnp.int32, (count, 1), 0) * devices + device
    live = jnp.concatenate(
        [
            jnp.where((row_in + part * packed) // BLK >= first_lane, 1.0, 0.0)
            for part in range(pack)
        ],
        axis=0,
    ).astype(jnp.float32)
    values = (values * live).astype(jnp.bfloat16)
    keep_lane = lane_of // (2 * fields) % 2 * fields + lane_of % fields
    keep = (
        lax.broadcasted_iota(jnp.int32, (hf, lanes), 0) == keep_lane
    ).astype(jnp.float32)
    down = lax.broadcasted_iota(jnp.int32, (lanes, width), 0)
    gather = (
        down // fields % 2 * waves + down // (4 * fields)
        == lax.broadcasted_iota(jnp.int32, (lanes, width), 1)
    ).astype(jnp.float32).astype(jnp.bfloat16)
    pick = (
        lax.broadcasted_iota(jnp.int32, (BLK, fields), 0) % fields
        == lax.broadcasted_iota(jnp.int32, (BLK, fields), 1)
    ).astype(jnp.float32).astype(jnp.bfloat16)
    across = (((1,), (1,)), ((), ()))
    half_mixer = lax.dot_general(
        pick, mixing_ref[...], across, preferred_element_type=jnp.float32
    ).astype(jnp.bfloat16)
    mixer = lax.dot_general(half_mixer, pick, across, preferred_element_type=jnp.float32)
    same = (
        lax.broadcasted_iota(jnp.int32, (BLK, BLK), 0) // fields
        == lax.broadcasted_iota(jnp.int32, (BLK, BLK), 1) // fields
    )
    mixer = jnp.where(same, mixer, 0.0).astype(jnp.bfloat16)
    mixed = jnp.concatenate(
        [
            jnp.dot(values[:, at : at + BLK], mixer, preferred_element_type=jnp.float32)
            for at in range(0, lanes, BLK)
        ],
        axis=1,
    )
    scale = (2.0 * waves) ** (-0.5)

    def fold(source):
        spread = (source[:, None, :] * keep[None, :, :]).reshape(rows * hf, lanes)
        return scale * jnp.dot(
            spread.astype(jnp.bfloat16), gather, preferred_element_type=jnp.float32
        )

    high = mixed.astype(jnp.bfloat16).astype(jnp.float32)
    straight, mix_high, mix_low = fold(values.astype(jnp.float32)), fold(high), fold(mixed - high)
    pairs = (
        jnp.concatenate([straight, jnp.zeros_like(straight)], axis=1),
        jnp.concatenate([mix_high, mix_low], axis=1),
    )
    for part, source in enumerate(pairs):
        for image in range(4):
            sign = signs[image]
            signed = source * jnp.concatenate([sign, sign], axis=1)
            at = (2 * image + part) * hf
            left[:rows, at : at + hf, :] = signed.reshape(rows, hf, 2 * width).astype(jnp.bfloat16)

    lane = lax.broadcasted_iota(jnp.int32, (1, span), 1)

    def proceed(state):
        return state[1]

    def advance(state):
        following, _, streams = state
        stages = []
        for row, index, cos_held, sin_held, sums in streams:
            quarter = lengths[jnp.minimum(row, rows - 1)] // 4
            at = jnp.minimum(row, rows - 1)
            fresh = index == 0
            cos_now = jnp.where(fresh, table_ref[at, 0:waves, :], cos_held)
            sin_now = jnp.where(fresh, table_ref[at, waves : 2 * waves, :], sin_held)
            step_cos = table_ref[at, 2 * waves : 3 * waves, :]
            step_sin = table_ref[at, 3 * waves : 4 * waves, :]
            cosines, sines = [], []
            for _ in range(TILES):
                cosines.append(cos_now)
                sines.append(-sin_now)
                cos_now, sin_now = (
                    cos_now * step_cos - sin_now * step_sin,
                    sin_now * step_cos + cos_now * step_sin,
                )
            phases = jnp.concatenate(
                [jnp.concatenate(cosines, axis=1), jnp.concatenate(sines, axis=1)], axis=0
            ).astype(jnp.bfloat16)
            stages.append((at, quarter, fresh, cos_now, sin_now, phases))
        grids = [
            jnp.dot(
                left[stage[0]],
                jnp.concatenate([stage[5], stage[5]], axis=0),
                preferred_element_type=jnp.float32,
            )
            for stage in stages
        ]
        added = []
        for stream, stage, grid in zip(streams, stages, grids):
            quarter, phases = stage[1], stage[5]
            position = lane + stream[1] * span
            share = jnp.where(
                (position == 0) | (position == quarter),
                0.5,
                jnp.where(position < quarter, 1.0, 0.0),
            ).astype(jnp.float32)
            columns = []
            for image in range(4):
                at = 2 * image * hf
                columns.append(
                    ((grid[at : at + hf] + jnp.tanh(grid[at + hf : at + 2 * hf])) * share).astype(
                        jnp.bfloat16
                    )
                )
            added.append(
                lax.dot_general(
                    jnp.concatenate(columns, axis=0),
                    phases,
                    (((1,), (1,)), ((), ())),
                    preferred_element_type=jnp.float32,
                )
            )
        later = []
        busy = jnp.bool_(False)
        for stream, stage, extra in zip(streams, stages, added):
            row, index, _, _, sums = stream
            sums = jnp.where(stage[2], 0.0, sums) + extra
            whole = sum(
                sums[image * hf : (image + 1) * hf] * signs[image]
                for image in range(4)
            )
            total[row] = whole
            done = (index + 1) * span > stage[1]
            idle = row >= rows
            taken = jnp.logical_and(done, jnp.logical_not(idle))
            row = jnp.where(taken, following, row)
            following = following - taken.astype(jnp.int32)
            row = jnp.where(row < 0, rows, row)
            index = jnp.where(done, 0, index + 1)
            busy = jnp.logical_or(busy, row < rows)
            later.append((row, index, stage[3], stage[4], sums))
        return following, busy, tuple(later)

    held = jnp.zeros((waves, BLK), jnp.float32)
    streams = tuple(
        (
            jnp.int32(rows - 1 - stream if stream < rows else rows),
            jnp.int32(0),
            held,
            held,
            jnp.zeros((4 * hf, width), jnp.float32),
        )
        for stream in range(STREAMS)
    )
    lax.while_loop(
        proceed, advance, (jnp.int32(rows - 1 - STREAMS), jnp.bool_(True), streams)
    )
    spread = lax.dot_general(
        (total[:rows] * weight_ref[...]).reshape(rows * hf, width).astype(jnp.bfloat16),
        gather,
        (((1,), (1,)), ((), ())),
        preferred_element_type=jnp.float32,
    )
    summed = jnp.sum(spread.reshape(rows, hf, lanes) * keep[None, :, :], axis=1)
    summed = summed * live
    for side in range(lat_count):
        out_ref[side] = jnp.concatenate(
            [
                summed[
                    part * count : (part + 1) * count, side * part_span : (side + 1) * part_span
                ]
                for part in range(pack)
            ],
            axis=1,
        ).astype(jnp.bfloat16)


def wave_tables(deal_list, lengths):
    rows, waves = lengths.shape[0], deal_list.shape[0]
    length = lengths.astype(jnp.float32)[:, None, None]
    wave = deal_list.astype(jnp.float32)[None, :, None]

    def angle_of(position):
        product = wave * position
        turned = product - jnp.floor(product / length) * length
        return turned * (2.0 * math.pi) / length

    inner = angle_of(jnp.arange(BLK, dtype=jnp.float32)[None, None, :])
    step = angle_of(jnp.full((1, 1, 1), float(BLK), jnp.float32))
    shape = (rows, waves, BLK)
    return jnp.concatenate(
        [
            jnp.cos(inner),
            jnp.sin(inner),
            jnp.broadcast_to(jnp.cos(step), shape),
            jnp.broadcast_to(jnp.sin(step), shape),
        ],
        axis=1,
    )


def rows_step(fourier, lengths, row_ids, deal_list, mixing, half_lat):
    fields, waves, rows = mixing.shape[0], deal_list.shape[0], row_ids.shape[0]
    hf, width = 2 * fields, 2 * waves
    pack = rows // fourier.shape[1]
    tables = wave_tables(deal_list, lengths)
    weight = jnp.sin(math.pi * (row_ids.astype(jnp.float32) + 0.5) / (2 * half_lat)) / jnp.sqrt(
        lengths.astype(jnp.float32)
    )
    vmem = pl.BlockSpec(memory_space=pltpu.VMEM)
    smem = pl.BlockSpec(memory_space=pltpu.SMEM)
    return pl.pallas_call(
        functools.partial(row_kernel, half_lat // pack),
        out_shape=jax.ShapeDtypeStruct(fourier.shape, jnp.bfloat16),
        in_specs=[smem, smem] + [vmem] * 4,
        out_specs=vmem,
        scratch_shapes=[
            pltpu.VMEM((rows, 8 * hf, 2 * width), jnp.bfloat16),
            pltpu.VMEM((rows + 1, hf, width), jnp.float32),
        ],
    )(lengths, deal_list, fourier, mixing, tables, weight[:, None, None])


def column_masks(pattern_ref, local_cols):
    slots, blocks_down, blocks = pattern_ref.shape
    column = lax.broadcasted_iota(jnp.int32, (1, local_cols), 1)
    column = column + lax.axis_index("lev") * local_cols
    odd = (1 - 2 * (column % 2)).astype(jnp.float32)
    masks = []
    for slot in range(slots):
        mask = jnp.zeros((1, local_cols), jnp.float32)
        for block in range(blocks):
            kept = pattern_ref[slot, blocks_down - 1, block].astype(jnp.float32)
            mask = jnp.where(column // BLK == block, kept, mask)
        masks.append(mask)
    return odd, masks


def peers_of(axis):
    count = lax.axis_size(axis)
    return [lax.rem(lax.axis_index(axis) + off, count) for off in range(1, count)]


def greet():
    barrier = pltpu.get_barrier_semaphore()
    total = 0
    for axis in ("lat", "lev"):
        for peer in peers_of(axis):
            pl.semaphore_signal(
                barrier, inc=1, device_id={axis: peer}, device_id_type=pl.DeviceIdType.MESH
            )
            total += 1
    pl.semaphore_wait(barrier, total)


def send(axis, sources, target, sems):
    copies = []
    for step, peer in enumerate(peers_of(axis)):
        copy = pltpu.make_async_remote_copy(
            src_ref=sources(peer),
            dst_ref=target,
            send_sem=sems.at[0, step],
            recv_sem=sems.at[1, step],
            device_id={axis: peer},
            device_id_type=pl.DeviceIdType.MESH,
        )
        copy.start()
        copies.append(copy)
    return copies


def inward_kernel(pack, pattern_ref, spec_ref, legendre_ref, out_ref, turned, leaving, arriving, summed, landed,
                  lev_sems, lat_sems):
    slots, _, half_lat = legendre_ref.shape
    lev_count, lat_count, count, width = leaving.shape
    devices = lev_count * lat_count
    lev_index, lat_index = lax.axis_index("lev"), lax.axis_index("lat")
    packed = half_lat // pack
    odd, masks = column_masks(pattern_ref, legendre_ref.shape[1])
    sums = []
    for slot in range(slots):
        kept = jnp.concatenate([spec_ref[slot, 0], spec_ref[slot, 1]], axis=0).astype(jnp.float32)
        kept = kept * masks[slot]
        sums.append(
            jnp.dot(
                jnp.concatenate([kept, kept * odd], axis=0).astype(jnp.bfloat16),
                legendre_ref[slot],
                preferred_element_type=jnp.float32,
            )
        )
    for block in range(packed // BLK):
        piece = jnp.concatenate(
            [
                value[:, part * packed + block * BLK : part * packed + (block + 1) * BLK]
                for part in range(pack)
                for value in sums
            ],
            axis=0,
        )
        turned[:, block * BLK : (block + 1) * BLK, :] = jnp.stack(
            [piece[at : at + BLK].T for at in range(0, width, BLK)]
        )
    for device in range(devices):
        for at in range(width // BLK):
            leaving[device // lat_count, device % lat_count, :, at * BLK : (at + 1) * BLK] = (
                turned[at, pl.ds(device, count, stride=devices), :].astype(jnp.bfloat16)
            )
    greet()
    copies = send("lev", lambda peer: leaving.at[peer], arriving.at[lev_index], lev_sems)
    mine = lev_index * lat_count
    total = jnp.stack(
        [
            jnp.concatenate(
                [
                    turned[at, pl.ds(mine + side, count, stride=devices), :]
                    for at in range(width // BLK)
                ],
                axis=1,
            )
            for side in range(lat_count)
        ]
    )
    for copy, peer in zip(copies, [lax.rem(lev_index + lev_count - off, lev_count) for off in range(1, lev_count)]):
        copy.wait_recv()
        total = total + arriving[peer].astype(jnp.float32)
    summed[...] = total.astype(jnp.bfloat16)
    crossing = send("lat", lambda peer: summed.at[peer], landed.at[lat_index], lat_sems)
    out_ref[lat_index] = summed[lat_index]
    for copy, peer in zip(crossing, [lax.rem(lat_index + lat_count - off, lat_count) for off in range(1, lat_count)]):
        copy.wait_recv()
        out_ref[peer] = landed[peer]
    for copy in copies + crossing:
        copy.wait_send()


def outward_kernel(pack, fields, pattern_ref, rows_ref, legendre_ref, out_ref, held, landed, gathered, turned,
                   lev_sems, lat_sems, load_sem):
    slots, local_cols, half_lat = held.shape
    lev_count, lat_count, count, width = gathered.shape
    devices = lev_count * lat_count
    lev_index, lat_index = lax.axis_index("lev"), lax.axis_index("lat")
    packed = half_lat // pack
    part_width = 4 * fields
    load = pltpu.make_async_copy(legendre_ref, held, load_sem)
    load.start()
    greet()
    crossing = send("lat", lambda peer: rows_ref.at[peer], landed.at[lat_index], lat_sems)
    landed[lat_index] = rows_ref[lat_index]
    for copy in crossing:
        copy.wait_recv()
    copies = send("lev", lambda peer: landed, gathered.at[lev_index], lev_sems)
    gathered[lev_index] = landed[...]
    for copy in copies:
        copy.wait_recv()
    for device in range(devices):
        block = gathered[device // lat_count, device % lat_count].astype(jnp.float32)
        for at in range(width // BLK):
            turned[at, pl.ds(device, count, stride=devices), :] = block[:, at * BLK : (at + 1) * BLK]
    load.wait()
    odd, masks = column_masks(pattern_ref, local_cols)
    sides = [turned[at].astype(jnp.bfloat16) for at in range(width // BLK)]
    for slot in range(slots):
        total = None
        for part in range(pack):
            at = part * slots * part_width + slot * part_width
            value = jnp.dot(
                held[slot, :, part * packed : (part + 1) * packed],
                sides[at // BLK],
                preferred_element_type=jnp.float32,
            )[:, at % BLK : at % BLK + part_width]
            total = value if total is None else total + value
        flat = total.T
        joined = flat[: 2 * fields] + odd * flat[2 * fields :]
        out_ref[slot] = joined * masks[slot]
    for copy in copies + crossing:
        copy.wait_send()


def local(spec_in, legendre, pattern, deal_list, circle_lengths, mixing):
    lat_index = lax.axis_index("lat")
    lev_index = lax.axis_index("lev")
    lat_count = lax.axis_size("lat")
    lev_count = lax.axis_size("lev")
    slots, local_cols, half_lat = legendre.shape
    fields = spec_in.shape[2]
    devices = lat_count * lev_count
    rows = half_lat // devices
    span = 4 * slots * fields
    pack = max(1, BLK // span)
    count, width = rows // pack, span * pack
    vmem = pl.BlockSpec(memory_space=pltpu.VMEM)
    block_shape = (lat_count, count, width)
    sems = [
        pltpu.SemaphoreType.DMA((2, lev_count)),
        pltpu.SemaphoreType.DMA((2, lat_count)),
    ]
    turned = pltpu.VMEM((width // BLK, half_lat // pack, BLK), jnp.float32)
    fourier = pl.pallas_call(
        functools.partial(inward_kernel, pack),
        out_shape=jax.ShapeDtypeStruct(block_shape, jnp.bfloat16),
        in_specs=[pl.BlockSpec(memory_space=pltpu.SMEM), vmem, vmem],
        out_specs=vmem,
        scratch_shapes=[
            turned,
            pltpu.VMEM((lev_count,) + block_shape, jnp.bfloat16),
            pltpu.VMEM((lev_count,) + block_shape, jnp.bfloat16),
            pltpu.VMEM(block_shape, jnp.bfloat16),
            pltpu.VMEM(block_shape, jnp.bfloat16),
        ]
        + sems,
        compiler_params=pltpu.CompilerParams(collective_id=0, has_side_effects=True),
    )(pattern, spec_in, legendre)
    row_ids = (
        jnp.arange(pack, dtype=jnp.int32)[:, None] * (half_lat // pack)
        + jnp.arange(count, dtype=jnp.int32)[None, :] * devices
        + (lev_index * lat_count + lat_index)
    ).reshape(rows)
    by_device = circle_lengths.reshape(rows, devices)
    chosen = jnp.arange(devices, dtype=jnp.int32)[None, :] == lev_index * lat_count + lat_index
    lengths = jnp.sum(jnp.where(chosen, by_device, 0), axis=1)
    leaving = rows_step(fourier, lengths, row_ids, deal_list, mixing, half_lat)
    product = pl.pallas_call(
        functools.partial(outward_kernel, pack, fields),
        out_shape=jax.ShapeDtypeStruct((slots, 2 * fields, local_cols), jnp.float32),
        in_specs=[
            pl.BlockSpec(memory_space=pltpu.SMEM),
            vmem,
            pl.BlockSpec(memory_space=pl.ANY),
        ],
        out_specs=vmem,
        scratch_shapes=[
            pltpu.VMEM(legendre.shape, jnp.bfloat16),
            pltpu.VMEM(block_shape, jnp.bfloat16),
            pltpu.VMEM((lev_count,) + block_shape, jnp.bfloat16),
            turned,
        ]
        + sems
        + [pltpu.SemaphoreType.DMA],
        compiler_params=pltpu.CompilerParams(collective_id=1, has_side_effects=True),
    )(pattern, leaving, legendre)
    return product.reshape(slots, 2, fields, local_cols)


def solution(mesh):
    return jax.shard_map(
        local,
        mesh=mesh,
        in_specs=(
            P("lat", None, None, "lev"),
            P("lat", "lev", None),
            P("lat", None, None),
            P(),
            P(),
            P(),
        ),
        out_specs=P("lat", None, None, "lev"),
        check_vma=False,
    )
```

```python
import functools
import math

import jax
import jax.numpy as jnp
from jax import lax
from jax.experimental import pallas as pl
from jax.experimental.pallas import tpu as pltpu
from jax.sharding import PartitionSpec as P

BLK = 128
TILES = 2
STREAMS = 12


def row_kernel(
    packed, lengths, deal, fourier_ref, mixing_ref, table_ref, weight_ref, out_ref, left, total
):
    lat_count, count, block_width = fourier_ref.shape
    rows = table_ref.shape[0]
    waves = table_ref.shape[1] // 4
    fields = mixing_ref.shape[0]
    hf, width = 2 * fields, 2 * waves
    pack = rows // count
    part_span = block_width // pack
    lanes = lat_count * part_span
    span = TILES * BLK
    devices = lat_count * lax.axis_size("lev")
    device = lax.axis_index("lev") * lat_count + lax.axis_index("lat")
    lane_of = lax.broadcasted_iota(jnp.int32, (1, lanes), 1)
    first_lane = jnp.zeros((1, lanes), jnp.int32)
    kind = lax.broadcasted_iota(jnp.int32, (1, width), 1)
    both = jnp.zeros((1, width), jnp.float32)
    for wave in range(waves):
        cut = deal[wave] * (pack * packed // BLK) // (2 * pack * packed)
        first_lane = jnp.where(lane_of // (4 * fields) == wave, cut, first_lane)
        odd = (1 - 2 * (deal[wave] % 2)).astype(jnp.float32)
        both = jnp.where(kind % waves == wave, odd, both)
    flip = jnp.where(kind < waves, 1.0, -1.0).astype(jnp.float32)
    signs = [jnp.ones_like(both), flip, both, both * flip]
    blocks = [fourier_ref[side].astype(jnp.float32) for side in range(lat_count)]
    values = jnp.concatenate(
        [
            jnp.concatenate(
                [block[:, part * part_span : (part + 1) * part_span] for block in blocks], axis=1
            )
            for part in range(pack)
        ],
        axis=0,
    )
    row_in = lax.broadcasted_iota(jnp.int32, (count, 1), 0) * devices + device
    live = jnp.concatenate(
        [
            jnp.where((row_in + part * packed) // BLK >= first_lane, 1.0, 0.0)
            for part in range(pack)
        ],
        axis=0,
    ).astype(jnp.float32)
    values = (values * live).astype(jnp.bfloat16)
    keep_lane = lane_of // (2 * fields) % 2 * fields + lane_of % fields
    keep = (
        lax.broadcasted_iota(jnp.int32, (hf, lanes), 0) == keep_lane
    ).astype(jnp.float32)
    down = lax.broadcasted_iota(jnp.int32, (lanes, width), 0)
    gather = (
        down // fields % 2 * waves + down // (4 * fields)
        == lax.broadcasted_iota(jnp.int32, (lanes, width), 1)
    ).astype(jnp.float32).astype(jnp.bfloat16)
    pick = (
        lax.broadcasted_iota(jnp.int32, (BLK, fields), 0) % fields
        == lax.broadcasted_iota(jnp.int32, (BLK, fields), 1)
    ).astype(jnp.float32).astype(jnp.bfloat16)
    across = (((1,), (1,)), ((), ()))
    half_mixer = lax.dot_general(
        pick, mixing_ref[...], across, preferred_element_type=jnp.float32
    ).astype(jnp.bfloat16)
    mixer = lax.dot_general(half_mixer, pick, across, preferred_element_type=jnp.float32)
    same = (
        lax.broadcasted_iota(jnp.int32, (BLK, BLK), 0) // fields
        == lax.broadcasted_iota(jnp.int32, (BLK, BLK), 1) // fields
    )
    mixer = jnp.where(same, mixer, 0.0).astype(jnp.bfloat16)
    mixed = jnp.concatenate(
        [
            jnp.dot(values[:, at : at + BLK], mixer, preferred_element_type=jnp.float32)
            for at in range(0, lanes, BLK)
        ],
        axis=1,
    )
    scale = (2.0 * waves) ** (-0.5)

    def fold(source):
        spread = (source[:, None, :] * keep[None, :, :]).reshape(rows * hf, lanes)
        return scale * jnp.dot(
            spread.astype(jnp.bfloat16), gather, preferred_element_type=jnp.float32
        )

    high = mixed.astype(jnp.bfloat16).astype(jnp.float32)
    straight, mix_high, mix_low = fold(values.astype(jnp.float32)), fold(high), fold(mixed - high)
    pairs = (
        jnp.concatenate([straight, jnp.zeros_like(straight)], axis=1),
        jnp.concatenate([mix_high, mix_low], axis=1),
    )
    for part, source in enumerate(pairs):
        for image in range(4):
            sign = signs[image]
            signed = source * jnp.concatenate([sign, sign], axis=1)
            at = (2 * image + part) * hf
            left[:rows, at : at + hf, :] = signed.reshape(rows, hf, 2 * width).astype(jnp.bfloat16)

    lane = lax.broadcasted_iota(jnp.int32, (1, span), 1)

    def proceed(state):
        return state[1]

    def advance(state):
        following, _, streams = state
        stages = []
        for row, index, cos_held, sin_held, sums in streams:
            quarter = lengths[jnp.minimum(row, rows - 1)] // 4
            at = jnp.minimum(row, rows - 1)
            fresh = index == 0
            cos_now = jnp.where(fresh, table_ref[at, 0:waves, :], cos_held)
            sin_now = jnp.where(fresh, table_ref[at, waves : 2 * waves, :], sin_held)
            step_cos = table_ref[at, 2 * waves : 3 * waves, :]
            step_sin = table_ref[at, 3 * waves : 4 * waves, :]
            cosines, sines = [], []
            for _ in range(TILES):
                cosines.append(cos_now)
                sines.append(-sin_now)
                cos_now, sin_now = (
                    cos_now * step_cos - sin_now * step_sin,
                    sin_now * step_cos + cos_now * step_sin,
                )
            phases = jnp.concatenate(
                [jnp.concatenate(cosines, axis=1), jnp.concatenate(sines, axis=1)], axis=0
            ).astype(jnp.bfloat16)
            stages.append((at, quarter, fresh, cos_now, sin_now, phases))
        grids = [
            jnp.dot(
                left[stage[0]],
                jnp.concatenate([stage[5], stage[5]], axis=0),
                preferred_element_type=jnp.float32,
            )
            for stage in stages
        ]
        added = []
        for stream, stage, grid in zip(streams, stages, grids):
            quarter, phases = stage[1], stage[5]
            position = lane + stream[1] * span
            share = jnp.where(
                (position == 0) | (position == quarter),
                0.5,
                jnp.where(position < quarter, 1.0, 0.0),
            ).astype(jnp.float32)
            columns = []
            for image in range(4):
                at = 2 * image * hf
                columns.append(
                    ((grid[at : at + hf] + jnp.tanh(grid[at + hf : at + 2 * hf])) * share).astype(
                        jnp.bfloat16
                    )
                )
            added.append(
                lax.dot_general(
                    jnp.concatenate(columns, axis=0),
                    phases,
                    (((1,), (1,)), ((), ())),
                    preferred_element_type=jnp.float32,
                )
            )
        later = []
        busy = jnp.bool_(False)
        for stream, stage, extra in zip(streams, stages, added):
            row, index, _, _, sums = stream
            sums = jnp.where(stage[2], 0.0, sums) + extra
            whole = sum(
                sums[image * hf : (image + 1) * hf] * signs[image]
                for image in range(4)
            )
            total[row] = whole
            done = (index + 1) * span > stage[1]
            idle = row >= rows
            taken = jnp.logical_and(done, jnp.logical_not(idle))
            row = jnp.where(taken, following, row)
            following = following - taken.astype(jnp.int32)
            row = jnp.where(row < 0, rows, row)
            index = jnp.where(done, 0, index + 1)
            busy = jnp.logical_or(busy, row < rows)
            later.append((row, index, stage[3], stage[4], sums))
        return following, busy, tuple(later)

    held = jnp.zeros((waves, BLK), jnp.float32)
    streams = tuple(
        (
            jnp.int32(rows - 1 - stream if stream < rows else rows),
            jnp.int32(0),
            held,
            held,
            jnp.zeros((4 * hf, width), jnp.float32),
        )
        for stream in range(STREAMS)
    )
    lax.while_loop(
        proceed, advance, (jnp.int32(rows - 1 - STREAMS), jnp.bool_(True), streams)
    )
    spread = lax.dot_general(
        (total[:rows] * weight_ref[...]).reshape(rows * hf, width).astype(jnp.bfloat16),
        gather,
        (((1,), (1,)), ((), ())),
        preferred_element_type=jnp.float32,
    )
    summed = jnp.sum(spread.reshape(rows, hf, lanes) * keep[None, :, :], axis=1)
    summed = summed * live
    for side in range(lat_count):
        out_ref[side] = jnp.concatenate(
            [
                summed[
                    part * count : (part + 1) * count, side * part_span : (side + 1) * part_span
                ]
                for part in range(pack)
            ],
            axis=1,
        ).astype(jnp.bfloat16)


def wave_tables(deal_list, lengths):
    rows, waves = lengths.shape[0], deal_list.shape[0]
    length = lengths.astype(jnp.float32)[:, None, None]
    wave = deal_list.astype(jnp.float32)[None, :, None]

    def angle_of(position):
        product = wave * position
        turned = product - jnp.floor(product / length) * length
        return turned * (2.0 * math.pi) / length

    inner = angle_of(jnp.arange(BLK, dtype=jnp.float32)[None, None, :])
    step = angle_of(jnp.full((1, 1, 1), float(BLK), jnp.float32))
    shape = (rows, waves, BLK)
    return jnp.concatenate(
        [
            jnp.cos(inner),
            jnp.sin(inner),
            jnp.broadcast_to(jnp.cos(step), shape),
            jnp.broadcast_to(jnp.sin(step), shape),
        ],
        axis=1,
    )


def rows_step(fourier, lengths, row_ids, deal_list, mixing, half_lat):
    fields, waves, rows = mixing.shape[0], deal_list.shape[0], row_ids.shape[0]
    hf, width = 2 * fields, 2 * waves
    pack = rows // fourier.shape[1]
    tables = wave_tables(deal_list, lengths)
    weight = jnp.sin(math.pi * (row_ids.astype(jnp.float32) + 0.5) / (2 * half_lat)) / jnp.sqrt(
        lengths.astype(jnp.float32)
    )
    vmem = pl.BlockSpec(memory_space=pltpu.VMEM)
    smem = pl.BlockSpec(memory_space=pltpu.SMEM)
    return pl.pallas_call(
        functools.partial(row_kernel, half_lat // pack),
        out_shape=jax.ShapeDtypeStruct(fourier.shape, jnp.bfloat16),
        in_specs=[smem, smem] + [vmem] * 4,
        out_specs=vmem,
        scratch_shapes=[
            pltpu.VMEM((rows, 8 * hf, 2 * width), jnp.bfloat16),
            pltpu.VMEM((rows + 1, hf, width), jnp.float32),
        ],
    )(lengths, deal_list, fourier, mixing, tables, weight[:, None, None])


def column_masks(pattern_ref, local_cols):
    slots, blocks_down, blocks = pattern_ref.shape
    column = lax.broadcasted_iota(jnp.int32, (1, local_cols), 1)
    column = column + lax.axis_index("lev") * local_cols
    odd = (1 - 2 * (column % 2)).astype(jnp.float32)
    masks = []
    for slot in range(slots):
        mask = jnp.zeros((1, local_cols), jnp.float32)
        for block in range(blocks):
            kept = pattern_ref[slot, blocks_down - 1, block].astype(jnp.float32)
            mask = jnp.where(column // BLK == block, kept, mask)
        masks.append(mask)
    return odd, masks


def peers_of(axis):
    count = lax.axis_size(axis)
    return [lax.rem(lax.axis_index(axis) + off, count) for off in range(1, count)]


def greet():
    expect(hail())


def expect(total):
    pl.semaphore_wait(pltpu.get_barrier_semaphore(), total)


def hail():
    barrier = pltpu.get_barrier_semaphore()
    total = 0
    for axis in ("lat", "lev"):
        for peer in peers_of(axis):
            pl.semaphore_signal(
                barrier, inc=1, device_id={axis: peer}, device_id_type=pl.DeviceIdType.MESH
            )
            total += 1
    return total


def send(axis, sources, target, sems):
    copies = []
    for step, peer in enumerate(peers_of(axis)):
        copy = pltpu.make_async_remote_copy(
            src_ref=sources(peer),
            dst_ref=target,
            send_sem=sems.at[0, step],
            recv_sem=sems.at[1, step],
            device_id={axis: peer},
            device_id_type=pl.DeviceIdType.MESH,
        )
        copy.start()
        copies.append(copy)
    return copies


def inward_kernel(pack, pattern_ref, spec_ref, legendre_ref, out_ref, turned, leaving, arriving, summed, landed,
                  lev_sems, lat_sems):
    slots, _, half_lat = legendre_ref.shape
    lev_count, lat_count, count, width = leaving.shape
    devices = lev_count * lat_count
    lev_index, lat_index = lax.axis_index("lev"), lax.axis_index("lat")
    packed = half_lat // pack
    greetings = hail()
    odd, masks = column_masks(pattern_ref, legendre_ref.shape[1])
    sums = []
    for slot in range(slots):
        kept = jnp.concatenate([spec_ref[slot, 0], spec_ref[slot, 1]], axis=0).astype(jnp.float32)
        kept = kept * masks[slot]
        sums.append(
            jnp.dot(
                jnp.concatenate([kept, kept * odd], axis=0).astype(jnp.bfloat16),
                legendre_ref[slot],
                preferred_element_type=jnp.float32,
            )
        )
    for block in range(packed // BLK):
        piece = jnp.concatenate(
            [
                value[:, part * packed + block * BLK : part * packed + (block + 1) * BLK]
                for part in range(pack)
                for value in sums
            ],
            axis=0,
        )
        turned[:, block * BLK : (block + 1) * BLK, :] = jnp.stack(
            [piece[at : at + BLK].T for at in range(0, width, BLK)]
        )
    for device in range(devices):
        for at in range(width // BLK):
            leaving[device // lat_count, device % lat_count, :, at * BLK : (at + 1) * BLK] = (
                turned[at, pl.ds(device, count, stride=devices), :].astype(jnp.bfloat16)
            )
    expect(greetings)
    copies = send("lev", lambda peer: leaving.at[peer], arriving.at[lev_index], lev_sems)
    mine = lev_index * lat_count
    total = jnp.stack(
        [
            jnp.concatenate(
                [
                    turned[at, pl.ds(mine + side, count, stride=devices), :]
                    for at in range(width // BLK)
                ],
                axis=1,
            )
            for side in range(lat_count)
        ]
    )
    for copy, peer in zip(copies, [lax.rem(lev_index + lev_count - off, lev_count) for off in range(1, lev_count)]):
        copy.wait_recv()
        total = total + arriving[peer].astype(jnp.float32)
    summed[...] = total.astype(jnp.bfloat16)
    crossing = send("lat", lambda peer: summed.at[peer], landed.at[lat_index], lat_sems)
    out_ref[lat_index] = summed[lat_index]
    for copy, peer in zip(crossing, [lax.rem(lat_index + lat_count - off, lat_count) for off in range(1, lat_count)]):
        copy.wait_recv()
        out_ref[peer] = landed[peer]
    for copy in copies + crossing:
        copy.wait_send()


def outward_kernel(pack, fields, pattern_ref, rows_ref, legendre_ref, out_ref, held, landed, gathered, turned,
                   lev_sems, lat_sems, load_sem):
    slots, local_cols, half_lat = held.shape
    lev_count, lat_count, count, width = gathered.shape
    devices = lev_count * lat_count
    lev_index, lat_index = lax.axis_index("lev"), lax.axis_index("lat")
    packed = half_lat // pack
    part_width = 4 * fields
    load = pltpu.make_async_copy(legendre_ref, held, load_sem)
    load.start()
    greet()
    crossing = send("lat", lambda peer: rows_ref.at[peer], landed.at[lat_index], lat_sems)
    landed[lat_index] = rows_ref[lat_index]
    for copy in crossing:
        copy.wait_recv()
    copies = send("lev", lambda peer: landed, gathered.at[lev_index], lev_sems)
    gathered[lev_index] = landed[...]
    for copy in copies:
        copy.wait_recv()
    for device in range(devices):
        block = gathered[device // lat_count, device % lat_count].astype(jnp.float32)
        for at in range(width // BLK):
            turned[at, pl.ds(device, count, stride=devices), :] = block[:, at * BLK : (at + 1) * BLK]
    load.wait()
    odd, masks = column_masks(pattern_ref, local_cols)
    sides = [turned[at].astype(jnp.bfloat16) for at in range(width // BLK)]
    for slot in range(slots):
        total = None
        for part in range(pack):
            at = part * slots * part_width + slot * part_width
            value = jnp.dot(
                held[slot, :, part * packed : (part + 1) * packed],
                sides[at // BLK],
                preferred_element_type=jnp.float32,
            )[:, at % BLK : at % BLK + part_width]
            total = value if total is None else total + value
        flat = total.T
        joined = flat[: 2 * fields] + odd * flat[2 * fields :]
        out_ref[slot] = joined * masks[slot]
    for copy in copies + crossing:
        copy.wait_send()


def local(spec_in, legendre, pattern, deal_list, circle_lengths, mixing):
    lat_index = lax.axis_index("lat")
    lev_index = lax.axis_index("lev")
    lat_count = lax.axis_size("lat")
    lev_count = lax.axis_size("lev")
    slots, local_cols, half_lat = legendre.shape
    fields = spec_in.shape[2]
    devices = lat_count * lev_count
    rows = half_lat // devices
    span = 4 * slots * fields
    pack = max(1, BLK // span)
    count, width = rows // pack, span * pack
    vmem = pl.BlockSpec(memory_space=pltpu.VMEM)
    block_shape = (lat_count, count, width)
    sems = [
        pltpu.SemaphoreType.DMA((2, lev_count)),
        pltpu.SemaphoreType.DMA((2, lat_count)),
    ]
    turned = pltpu.VMEM((width // BLK, half_lat // pack, BLK), jnp.float32)
    fourier = pl.pallas_call(
        functools.partial(inward_kernel, pack),
        out_shape=jax.ShapeDtypeStruct(block_shape, jnp.bfloat16),
        in_specs=[pl.BlockSpec(memory_space=pltpu.SMEM), vmem, vmem],
        out_specs=vmem,
        scratch_shapes=[
            turned,
            pltpu.VMEM((lev_count,) + block_shape, jnp.bfloat16),
            pltpu.VMEM((lev_count,) + block_shape, jnp.bfloat16),
            pltpu.VMEM(block_shape, jnp.bfloat16),
            pltpu.VMEM(block_shape, jnp.bfloat16),
        ]
        + sems,
        compiler_params=pltpu.CompilerParams(collective_id=0, has_side_effects=True),
    )(pattern, spec_in, legendre)
    row_ids = (
        jnp.arange(pack, dtype=jnp.int32)[:, None] * (half_lat // pack)
        + jnp.arange(count, dtype=jnp.int32)[None, :] * devices
        + (lev_index * lat_count + lat_index)
    ).reshape(rows)
    by_device = circle_lengths.reshape(rows, devices)
    chosen = jnp.arange(devices, dtype=jnp.int32)[None, :] == lev_index * lat_count + lat_index
    lengths = jnp.sum(jnp.where(chosen, by_device, 0), axis=1)
    leaving = rows_step(fourier, lengths, row_ids, deal_list, mixing, half_lat)
    product = pl.pallas_call(
        functools.partial(outward_kernel, pack, fields),
        out_shape=jax.ShapeDtypeStruct((slots, 2 * fields, local_cols), jnp.float32),
        in_specs=[
            pl.BlockSpec(memory_space=pltpu.SMEM),
            vmem,
            pl.BlockSpec(memory_space=pl.ANY),
        ],
        out_specs=vmem,
        scratch_shapes=[
            pltpu.VMEM(legendre.shape, jnp.bfloat16),
            pltpu.VMEM(block_shape, jnp.bfloat16),
            pltpu.VMEM((lev_count,) + block_shape, jnp.bfloat16),
            turned,
        ]
        + sems
        + [pltpu.SemaphoreType.DMA],
        compiler_params=pltpu.CompilerParams(collective_id=1, has_side_effects=True),
    )(pattern, leaving, legendre)
    return product.reshape(slots, 2, fields, local_cols)


def solution(mesh):
    return jax.shard_map(
        local,
        mesh=mesh,
        in_specs=(
            P("lat", None, None, "lev"),
            P("lat", "lev", None),
            P("lat", None, None),
            P(),
            P(),
            P(),
        ),
        out_specs=P("lat", None, None, "lev"),
        check_vma=False,
    )
```
